256 devices in a mesh: dp: 128 (over y, z, x), tensor: 2 (over core).
Axes of the slice: x: 4, y: 4, z: 8, core: 2. Of those that a mesh axis runs over, the one named last changes fastest.
Arguments:
- queries: bfloat16 [16384, 4096], P('dp', 'tensor'), may hold values from -4 to 4
- cached_key_rows: bfloat16 [256, 1024, 1024], P('dp', None, 'tensor'), may hold values from -1 to 1
- cached_value_rows: bfloat16 [256, 1024, 1024], P('dp', None, 'tensor'), may hold values from -6 to 6
- parent_ids: int32 [16384], P('dp'), may hold values from 0 to 255, as said below
- lengths: int32 [256], P('dp'), may hold values from 128 to 1024
- residual: bfloat16 [16384, 2048], P('dp', 'tensor'), may hold values from -4 to 4
- out_weight: bfloat16 [4096, 2048], P('tensor'), may hold values from -0.09375 to 0.09375
Outputs:
- mixed_out: bfloat16 [16384, 2048], P('dp', 'tensor')
The draws below stay inside these ranges and needn't reach their ends.
Inputs may be any that keep to these rules, and one draw needn't show every extreme that they name: `parent_ids`: among the 128 children of one index of dp (aligned blocks), at most 2 have parents of one owner; in every draw one owner has exactly 2 children from every block.
All inputs are finite; a program needn't handle non-finite values.
Results may differ from the reference program's by a relative error of at most 0.0044.
Values may be sent and summed in bfloat16 or wider, within the bound.
No kernel may reach another device: no remote copies, remote signals or barrier semaphores. Data moves between devices by JAX's collectives and lax.ppermute only.
A program may use at most 64 MiB of HBM per device.

```python
import math
import jax
import jax.numpy as jnp
from jax import lax

QUERY_HEADS = 32
KEY_VALUE_HEADS = 8
HEAD_WIDTH = 128
W = 2048
CH_DEV = 128
LONGEST_PREFIX = 1024
PAR_DEV = 2
CAP = 2
CHILDREN = 16384
PARENT_COUNT = 256


def draw_parent_ids(key, part):
    owner_count = PARENT_COUNT // PAR_DEV
    first_key, second_key = jax.random.split(jax.random.fold_in(key, 11))
    busy_owner = jax.random.randint(first_key, (), 0, owner_count)

    def one_block(block_key):
        perm_key, order_key, sub_key = jax.random.split(block_key, 3)
        tokens = jax.random.permutation(perm_key, (owner_count - 1) * CAP)[:CH_DEV - CAP]
        others = tokens // CAP
        others = others + (others >= busy_owner).astype(jnp.int32)
        owners = jnp.concatenate([jnp.full((CAP,), busy_owner, jnp.int32), others.astype(jnp.int32)])
        owners = jax.random.permutation(order_key, owners)
        sub_index = jax.random.randint(sub_key, (CH_DEV,), 0, PAR_DEV)
        return owners * PAR_DEV + sub_index
    block_keys = jax.random.split(second_key, owner_count)
    return jax.vmap(one_block)(block_keys).reshape(-1).astype(jnp.int32)


def draw_lengths(key, part):
    first_key, second_key = jax.random.split(jax.random.fold_in(key, 29))
    prefix_lengths = jax.random.randint(first_key, (PARENT_COUNT,), LONGEST_PREFIX // 8, LONGEST_PREFIX + 1)
    longest = jax.random.randint(second_key, (), 0, PARENT_COUNT)
    prefix_lengths = jnp.where(jnp.arange(PARENT_COUNT) == longest, LONGEST_PREFIX, prefix_lengths)
    return prefix_lengths.astype(jnp.int32)


def levels(own_key, shape, cuts, smallest, high):
    def one(axis_at, parts):
        draws = jax.random.uniform(jax.random.fold_in(jax.random.fold_in(own_key, 6), axis_at), (parts,), jnp.float32, smallest / len(cuts), high / len(cuts))
        return jnp.repeat(jnp.exp(draws), shape[axis_at] // parts).reshape((-1,) + (1,) * (len(shape) - axis_at - 1))

    factor_of = one(*cuts[0])
    for cut in cuts[1:]:
        factor_of = factor_of * one(*cut)
    return factor_of


def gaussian(stream_key, shape, scale, most, shards=(), held_as=jnp.bfloat16):
    level = levels(stream_key, shape, shards, -0.22, 0.18) if shards else 1.0
    result = jax.random.normal(stream_key, shape, jnp.float32) * scale * level
    return jnp.minimum(jnp.maximum(result, -most), most).astype(held_as)


def setup_inputs(seed: int = 0) -> dict:
    seeds = jax.random.split(jax.random.key(seed), 8)
    queries = jnp.clip(jax.random.uniform(seeds[0], (CHILDREN, QUERY_HEADS * HEAD_WIDTH), jnp.float32, -4.0, 4.0) * levels(seeds[0], (CHILDREN, QUERY_HEADS * HEAD_WIDTH), ((0, 128), (1, 2)), -0.4, 0.0), -4.0, 4.0).astype(jnp.bfloat16)
    cached_key_rows = jnp.clip(jax.random.uniform(seeds[1], (PARENT_COUNT, LONGEST_PREFIX, KEY_VALUE_HEADS * HEAD_WIDTH), jnp.float32, -1.0, 1.0) * levels(seeds[1], (PARENT_COUNT, LONGEST_PREFIX, KEY_VALUE_HEADS * HEAD_WIDTH), ((0, 128), (2, 2)), -0.4, 0.0), -1.0, 1.0).astype(jnp.bfloat16)
    cached_value_rows = gaussian(seeds[2], (PARENT_COUNT, LONGEST_PREFIX, KEY_VALUE_HEADS * HEAD_WIDTH), 1.0, 6.0, ((0, 128), (2, 2)))
    parent_ids = draw_parent_ids(jax.random.fold_in(seeds[7], 71), 0)
    lengths = draw_lengths(jax.random.fold_in(seeds[7], 71), 0)
    residual = gaussian(seeds[5], (CHILDREN, W), 0.5, 4.0, ((0, 128), (1, 2)))
    out_weight = gaussian(seeds[6], (QUERY_HEADS * HEAD_WIDTH, W), (QUERY_HEADS * HEAD_WIDTH) ** -0.5, 0.09375, ((0, 2),))
    return dict(queries=queries, cached_key_rows=cached_key_rows, cached_value_rows=cached_value_rows, parent_ids=parent_ids, lengths=lengths, residual=residual, out_weight=out_weight)


def reference(queries, cached_key_rows, cached_value_rows, parent_ids, lengths, residual, out_weight):
    group_width = QUERY_HEADS // KEY_VALUE_HEADS
    score_scale = 1.0 / math.sqrt(HEAD_WIDTH)
    block_length = math.gcd(CHILDREN, 64)
    positions = jnp.arange(LONGEST_PREFIX, dtype=jnp.int32)

    def attend(operands):
        query_matrix, parent_nodes = operands
        key_matrix = cached_key_rows[parent_nodes].astype(jnp.float32).reshape(block_length, LONGEST_PREFIX, KEY_VALUE_HEADS, HEAD_WIDTH)
        value_matrix = cached_value_rows[parent_nodes].astype(jnp.float32).reshape(block_length, LONGEST_PREFIX, KEY_VALUE_HEADS, HEAD_WIDTH)
        limits = lengths[parent_nodes]
        query_head_count = query_matrix.astype(jnp.float32).reshape(block_length, KEY_VALUE_HEADS, group_width, HEAD_WIDTH)
        scores = jnp.einsum('bjgd,bljd->bjgl', query_head_count, key_matrix) * score_scale
        live_mask = positions[None, :] < limits[:, None]
        raised = jnp.where(live_mask[:, None, None, :], jnp.exp(scores), jnp.zeros((), jnp.float32))
        totals = lax.optimization_barrier(jnp.sum(raised, axis=-1))
        rounded = lax.optimization_barrier(raised.astype(jnp.bfloat16)).astype(jnp.float32)
        summed = jnp.einsum('bjgl,bljd->bjgd', rounded, value_matrix)
        return (summed / totals[..., None]).reshape(block_length, QUERY_HEADS * HEAD_WIDTH).astype(jnp.bfloat16)
    attended = lax.map(attend, (queries.reshape(CHILDREN // block_length, block_length, QUERY_HEADS * HEAD_WIDTH), parent_ids.reshape(CHILDREN // block_length, block_length)))
    attended = attended.reshape(CHILDREN, QUERY_HEADS * HEAD_WIDTH)
    mixed_out = residual.astype(jnp.float32) + jnp.dot(attended, out_weight, preferred_element_type=jnp.float32)
    return mixed_out.astype(jnp.bfloat16)
```

```python
import math

import jax
import jax.numpy as jnp
from jax import lax
from jax.experimental import pallas as pl
from jax.experimental.pallas import tpu as pltpu
from jax.sharding import PartitionSpec as P

HEAD_WIDTH = 128
LANES = 128
CHUNK = 64

F32 = jnp.float32
BF16 = jnp.bfloat16
VMEM = pl.BlockSpec(memory_space=pltpu.VMEM)
SMEM = pl.BlockSpec(memory_space=pltpu.SMEM)
ANY = pl.BlockSpec(memory_space=pl.ANY)
PARAMS = pltpu.CompilerParams(vmem_limit_bytes=56 * 1024 * 1024)


def iota(shape, dim):
    return lax.broadcasted_iota(jnp.int32, shape, dim)


def one_hot(flags):
    return jnp.where(flags, 1.0, 0.0).astype(BF16)


def product(left, right):
    return jnp.dot(left, right, preferred_element_type=F32)


def as_column(row):
    n = row.shape[1]
    eye = iota((n, n), 0) == iota((n, n), 1)
    return jnp.sum(jnp.where(eye, row, 0.0), axis=1, keepdims=True)


def as_row(column):
    n = column.shape[0]
    eye = iota((n, n), 0) == iota((n, n), 1)
    return jnp.sum(jnp.where(eye, column, 0.0), axis=0, keepdims=True)


def owners(ids, parents_here):
    shift = parents_here.bit_length() - 1
    owner = lax.shift_right_logical(ids, shift)
    return owner.astype(F32), (ids - lax.shift_left(owner, shift)).astype(F32)


def send_kernel(capacity, kv_heads, parents_here, ids_ref, queries_ref, out_ref):
    children = queries_ref.shape[0]
    width = queries_ref.shape[1] // kv_heads
    rows = out_ref.shape[0]
    owner, sub = owners(ids_ref[...], parents_here)
    owner_column = as_column(owner)
    square = (children, children)
    earlier = (owner_column == owner) & (iota(square, 0) < iota(square, 1))
    rank = jnp.sum(jnp.where(earlier, 1.0, 0.0), axis=0, keepdims=True)
    slot = (owner * capacity + rank).astype(jnp.int32)
    row = iota((rows, children), 0)
    shift = kv_heads.bit_length() - 1
    here = lax.shift_right_logical(row, shift) == slot
    head = row & (kv_heads - 1)
    placing = jnp.concatenate([one_hot(here & (head == j)) for j in range(kv_heads)], axis=1)
    stacked = jnp.concatenate(
        [queries_ref[:, j * width : (j + 1) * width] for j in range(kv_heads)], axis=0
    )
    out_ref[:, :width] = product(placing, stacked).astype(BF16)
    mark = jnp.broadcast_to(as_column(sub) + 1.0, (children, LANES)).astype(BF16)
    out_ref[:, width:] = product(one_hot(here), mark).astype(BF16)


def attend_kernel(
    capacity, kv_heads, lengths_ref, arrived_ref, keys_hbm, values_hbm, weight_hbm,
    attended_ref, partial_ref, keys, values, weight, natural, ordered, answered, sems,
):
    parents_here, prefix, _ = keys.shape
    sources = arrived_ref.shape[0] // (capacity * kv_heads)
    slots = sources * capacity
    width = arrived_ref.shape[1] - LANES
    group = width // HEAD_WIDTH
    half = weight.shape[1]
    other = pl.multiple_of((1 - lax.axis_index("tensor")) * half, half)
    copies = (
        pltpu.make_async_copy(keys_hbm, keys, sems.at[0]),
        pltpu.make_async_copy(values_hbm, values, sems.at[1]),
        pltpu.make_async_copy(weight_hbm.at[:, pl.ds(other, half)], weight, sems.at[2]),
    )
    for copy in copies:
        copy.start()
    rows = arrived_ref.shape[0]
    for j in range(kv_heads):
        place = iota((slots, rows), 0)
        source = place & (sources - 1)
        rank = lax.shift_right_logical(place, sources.bit_length() - 1)
        picked = one_hot(
            iota((slots, rows), 1) == source * (capacity * kv_heads) + rank * kv_heads + j
        )
        if j == 0:
            found = product(picked, arrived_ref[...])
            natural[:, :width] = found[:, :width].astype(BF16)
            marks = found[:, width:]
        else:
            natural[:, j * width : (j + 1) * width] = product(
                picked, arrived_ref[:, :width]
            ).astype(BF16)
    before = one_hot(iota((slots, slots), 0) > iota((slots, slots), 1))
    position = jnp.full((slots, LANES), -1.0, F32)
    start = jnp.int32(0)
    ends = []
    for parent in range(parents_here):
        mine = marks == parent + 1.0
        ahead = product(before, one_hot(mine))
        position = jnp.where(mine, ahead + start.astype(F32), position)
        count = (jnp.sum(jnp.where(mine, 1.0, 0.0)) * (1.0 / LANES)).astype(jnp.int32)
        start = start + lax.shift_left(
            lax.shift_right_logical(count + (CHUNK - 1), CHUNK.bit_length() - 1),
            CHUNK.bit_length() - 1,
        )
        ends.append(start)
    position_row = jnp.concatenate(
        [as_row(position[k * sources : (k + 1) * sources]) for k in range(capacity)], axis=1
    ).astype(jnp.int32)
    places = ordered.shape[0]
    ordering = one_hot(iota((places, slots), 0) == position_row)
    ordered[...] = product(ordering, natural[...]).astype(BF16)
    answered[...] = jnp.zeros_like(answered)
    copies[0].wait()
    copies[1].wait()
    factor = (1.0 / math.sqrt(HEAD_WIDTH)) * math.log2(math.e)

    def chunk_step(index, carry):
        base = pl.multiple_of(index * CHUNK, CHUNK)
        parent = jnp.int32(0)
        for end in ends[:-1]:
            parent = parent + (base >= end).astype(jnp.int32)
        live = iota((CHUNK * group, prefix), 1) < lengths_ref[parent]
        for j in range(kv_heads):
            block = ordered[pl.ds(base, CHUNK), j * width : (j + 1) * width]
            heads = jnp.concatenate(
                [block[:, g * HEAD_WIDTH : (g + 1) * HEAD_WIDTH] for g in range(group)], axis=0
            )
            columns = slice(j * HEAD_WIDTH, (j + 1) * HEAD_WIDTH)
            scores = lax.dot_general(
                heads, keys[parent, :, columns], (((1,), (1,)), ((), ())),
                preferred_element_type=F32,
            )
            raised = jnp.where(live, jnp.exp2(scores * factor), 0.0)
            totals = jnp.sum(raised, axis=1, keepdims=True)
            summed = product(raised.astype(BF16), values[parent, :, columns])
            scaled = (summed / totals).astype(BF16)
            for g in range(group):
                answered[
                    pl.ds(base, CHUNK),
                    j * width + g * HEAD_WIDTH : j * width + (g + 1) * HEAD_WIDTH,
                ] = scaled[g * CHUNK : (g + 1) * CHUNK]
        return carry

    lax.fori_loop(0, lax.shift_right_logical(start, CHUNK.bit_length() - 1), chunk_step, 0)
    lane = iota((slots, places), 1).astype(F32)
    back = one_hot(lane == position[:, :1])
    attended_ref[...] = product(back, answered[...]).astype(BF16)
    copies[2].wait()
    partial_ref[...] = product(attended_ref[...], weight[...]).astype(BF16)


def project_kernel(attended_ref, weight_hbm, out_ref, weight, sems):
    half = weight.shape[1]
    mine = pl.multiple_of(lax.axis_index("tensor") * half, half)
    parts = sems.shape[0]
    depth = weight.shape[0] // parts
    copies = [
        pltpu.make_async_copy(
            weight_hbm.at[pl.ds(i * depth, depth), pl.ds(mine, half)],
            weight.at[pl.ds(i * depth, depth)],
            sems.at[i],
        )
        for i in range(parts)
    ]
    for copy in copies:
        copy.start()
    for i, copy in enumerate(copies):
        copy.wait()
        rows = slice(i * depth, (i + 1) * depth)
        term = product(attended_ref[:, rows], weight[rows])
        out_ref[...] = term if i == 0 else out_ref[...] + term


def answer_kernel(capacity, parts, mine_ref, other_ref, out_ref):
    slots, columns = mine_ref.shape
    sources = slots // capacity
    width = columns // parts
    rows = out_ref.shape[0]
    total = (mine_ref[...] + other_ref[...].astype(F32)).astype(BF16)
    row = iota((rows, slots), 0)
    part = row & (parts - 1)
    slot = lax.shift_right_logical(row, parts.bit_length() - 1)
    rank = slot & (capacity - 1)
    source = lax.shift_right_logical(slot, capacity.bit_length() - 1)
    here = iota((rows, slots), 1) == rank * sources + source
    sent = jnp.zeros((rows, width), F32)
    for i in range(parts):
        sent = sent + product(
            one_hot(here & (part == i)), total[:, i * width : (i + 1) * width]
        )
    out_ref[...] = sent.astype(BF16)


def mix_kernel(capacity, parts, parents_here, ids_ref, returned_ref, residual_ref, out_ref):
    children, columns = residual_ref.shape
    width = columns // parts
    rows = returned_ref.shape[0]
    owner, _ = owners(ids_ref[...], parents_here)
    owner_column = as_column(owner)
    square = (children, children)
    earlier = (owner_column == owner) & (iota(square, 1) < iota(square, 0))
    rank = jnp.sum(jnp.where(earlier, 1.0, 0.0), axis=1, keepdims=True)
    slot = (owner_column * capacity + rank).astype(jnp.int32)
    row = iota((children, rows), 1)
    here = lax.shift_right_logical(row, parts.bit_length() - 1) == slot
    part = row & (parts - 1)
    for i in range(parts):
        columns_here = slice(i * width, (i + 1) * width)
        found = product(one_hot(here & (part == i)), returned_ref[...])
        out_ref[:, columns_here] = (
            residual_ref[:, columns_here].astype(F32) + found
        ).astype(BF16)


def local(queries, cached_key_rows, cached_value_rows, parent_ids, lengths, residual, out_weight):
    dp_count = lax.axis_size("dp")
    tensor_count = lax.axis_size("tensor")
    children, columns = queries.shape
    parents_here, prefix, key_columns = cached_key_rows.shape
    kv_heads = key_columns // HEAD_WIDTH
    capacity = max(2, 2 * children // dp_count)
    slots = dp_count * capacity
    width = columns // kv_heads
    message = capacity * kv_heads
    half = out_weight.shape[1] // tensor_count
    parts = 8 // capacity
    ids = parent_ids.reshape(1, children)
    outgoing = pl.pallas_call(
        lambda *refs: send_kernel(capacity, kv_heads, parents_here, *refs),
        out_shape=jax.ShapeDtypeStruct((dp_count * message, width + LANES), BF16),
        in_specs=[VMEM, VMEM],
        out_specs=VMEM,
        compiler_params=PARAMS,
        name="send",
    )(ids, queries)
    arrived = lax.all_to_all(
        outgoing.reshape(dp_count, message, width + LANES), "dp", 0, 0, tiled=True
    ).reshape(dp_count * message, width + LANES)
    places = slots + (parents_here - 1) * CHUNK
    attended, partial_value = pl.pallas_call(
        lambda *refs: attend_kernel(capacity, kv_heads, *refs),
        out_shape=(
            jax.ShapeDtypeStruct((slots, columns), BF16),
            jax.ShapeDtypeStruct((slots, half), BF16),
        ),
        in_specs=[SMEM, VMEM, ANY, ANY, ANY],
        out_specs=(VMEM, VMEM),
        scratch_shapes=[
            pltpu.VMEM((parents_here, prefix, key_columns), BF16),
            pltpu.VMEM((parents_here, prefix, key_columns), BF16),
            pltpu.VMEM((columns, half), BF16),
            pltpu.VMEM((slots, columns), BF16),
            pltpu.VMEM((places, columns), BF16),
            pltpu.VMEM((places, columns), BF16),
            pltpu.SemaphoreType.DMA((3,)),
        ],
        compiler_params=PARAMS,
        name="attend",
    )(lengths, arrived, cached_key_rows, cached_value_rows, out_weight)
    other = lax.ppermute(partial_value, "tensor", [(0, 1), (1, 0)])
    mine = pl.pallas_call(
        project_kernel,
        out_shape=jax.ShapeDtypeStruct((slots, half), F32),
        in_specs=[VMEM, ANY],
        out_specs=VMEM,
        scratch_shapes=[pltpu.VMEM((columns, half), BF16), pltpu.SemaphoreType.DMA((4,))],
        compiler_params=PARAMS,
        cost_estimate=pl.CostEstimate(
            flops=2 * slots * columns * half, bytes_accessed=2 * columns * half, transcendentals=0
        ),
        name="project",
    )(attended, out_weight)
    answers = pl.pallas_call(
        lambda *refs: answer_kernel(capacity, parts, *refs),
        out_shape=jax.ShapeDtypeStruct((slots * parts, half // parts), BF16),
        in_specs=[VMEM, VMEM],
        out_specs=VMEM,
        compiler_params=PARAMS,
        name="answer",
    )(mine, other)
    returned = lax.all_to_all(
        answers.reshape(dp_count, capacity * parts, half // parts), "dp", 0, 0, tiled=True
    ).reshape(slots * parts, half // parts)
    return pl.pallas_call(
        lambda *refs: mix_kernel(capacity, parts, parents_here, *refs),
        out_shape=jax.ShapeDtypeStruct(residual.shape, BF16),
        in_specs=[VMEM, VMEM, VMEM],
        out_specs=VMEM,
        compiler_params=PARAMS,
        name="mix",
    )(ids, returned, residual)


def solution(mesh):
    placed = (
        P("dp", "tensor"),
        P("dp", None, "tensor"),
        P("dp", None, "tensor"),
        P("dp"),
        P("dp"),
        P("dp", "tensor"),
        P("tensor", None),
    )
    return jax.shard_map(
        local, mesh=mesh, in_specs=placed, out_specs=P("dp", "tensor"), check_vma=False
    )
```

```python
import math

import jax
import jax.numpy as jnp
from jax import lax
from jax.experimental import pallas as pl
from jax.experimental.pallas import tpu as pltpu
from jax.sharding import PartitionSpec as P

HEAD_WIDTH = 128
LANES = 128
CHUNK = 64

F32 = jnp.float32
BF16 = jnp.bfloat16
VMEM = pl.BlockSpec(memory_space=pltpu.VMEM)
SMEM = pl.BlockSpec(memory_space=pltpu.SMEM)
HBM = pl.BlockSpec(memory_space=pltpu.HBM)
def params(mib):
    return pltpu.CompilerParams(vmem_limit_bytes=mib * 1024 * 1024)


def iota(shape, dim):
    return lax.broadcasted_iota(jnp.int32, shape, dim)


def one_hot(flags):
    return jnp.where(flags, 1.0, 0.0).astype(BF16)


def product(left, right):
    return jnp.dot(left, right, preferred_element_type=F32)


def as_column(row):
    n = row.shape[1]
    eye = iota((n, n), 0) == iota((n, n), 1)
    return jnp.sum(jnp.where(eye, row, 0.0), axis=1, keepdims=True)


def as_row(column):
    n = column.shape[0]
    eye = iota((n, n), 0) == iota((n, n), 1)
    return jnp.sum(jnp.where(eye, column, 0.0), axis=0, keepdims=True)


def owners(ids, parents_here):
    shift = parents_here.bit_length() - 1
    owner = lax.shift_right_logical(ids, shift)
    return owner.astype(F32), (ids - lax.shift_left(owner, shift)).astype(F32)


def slots_of(ids, parents_here, capacity):
    children = ids.shape[1]
    owner, sub = owners(ids, parents_here)
    square = (children, children)
    earlier = (as_column(owner) == owner) & (iota(square, 0) < iota(square, 1))
    rank = jnp.sum(jnp.where(earlier, 1.0, 0.0), axis=0, keepdims=True)
    return owner * capacity + rank, sub


def send_kernel(capacity, parents_here, ids_ref, queries_ref, out_ref):
    children, columns = queries_ref.shape
    slot, sub = slots_of(ids_ref[...], parents_here, capacity)
    placing = one_hot(iota((out_ref.shape[0], children), 0) == slot.astype(jnp.int32))
    out_ref[:, :columns] = product(placing, queries_ref[...]).astype(BF16)
    mark = jnp.broadcast_to(as_column(sub) + 1.0, (children, LANES)).astype(BF16)
    out_ref[:, columns:] = product(placing, mark).astype(BF16)


def prepare_kernel(lengths_ref, keys_ref, values_ref, turned_ref, valued_ref):
    parents_here, prefix, columns = keys_ref.shape
    for parent in range(parents_here):
        live = iota((prefix, HEAD_WIDTH), 0) < lengths_ref[parent]
        counted = jnp.where(live, 1.0, 0.0).astype(BF16)
        for j in range(columns // HEAD_WIDTH):
            head = slice(j * HEAD_WIDTH, (j + 1) * HEAD_WIDTH)
            turned_ref[parent, j] = keys_ref[parent, :, head].T
            valued_ref[parent, j, :, :HEAD_WIDTH] = jnp.where(
                live, values_ref[parent, :, head].astype(F32), 0.0
            ).astype(BF16)
            valued_ref[parent, j, :, HEAD_WIDTH:] = counted


def attend_kernel(
    lengths_ref, arrived_ref, turned_ref, valued_hbm, weight_hbm,
    attended_ref, partial_ref, mine_ref, valued_ref, weight_ref, ordered, answered, sems,
):
    parents_here, kv_heads, _, prefix = turned_ref.shape
    slots, columns = attended_ref.shape
    width = columns // kv_heads
    group = width // HEAD_WIDTH
    half = partial_ref.shape[1]
    core = lax.axis_index("tensor")
    mine = pl.multiple_of(core * half, half)
    other = pl.multiple_of((1 - core) * half, half)
    copies = (
        pltpu.make_async_copy(valued_hbm, valued_ref, sems.at[0]),
        pltpu.make_async_copy(weight_hbm.at[:, pl.ds(other, half)], weight_ref, sems.at[1]),
        pltpu.make_async_copy(weight_hbm.at[:, pl.ds(mine, half)], mine_ref, sems.at[2]),
    )
    copies[0].start()
    arrived = arrived_ref[...].reshape(slots, arrived_ref.shape[2])
    marks = arrived[:, columns:].astype(F32)
    before = one_hot(iota((slots, slots), 0) > iota((slots, slots), 1))
    position = jnp.full((slots, LANES), -1.0, F32)
    start = jnp.int32(0)
    ends = []
    for parent in range(parents_here):
        mine = marks == parent + 1.0
        ahead = product(before, one_hot(mine))
        position = jnp.where(mine, ahead + start.astype(F32), position)
        count = (jnp.sum(jnp.where(mine, 1.0, 0.0)) * (1.0 / LANES)).astype(jnp.int32)
        start = start + lax.shift_left(
            lax.shift_right_logical(count + (CHUNK - 1), CHUNK.bit_length() - 1),
            CHUNK.bit_length() - 1,
        )
        ends.append(start)
    position_row = jnp.concatenate(
        [as_row(position[i : i + LANES]) for i in range(0, slots, LANES)], axis=1
    ).astype(jnp.int32)
    places = ordered.shape[0]
    ordering = one_hot(iota((places, slots), 0) == position_row)
    ordered[...] = product(ordering, arrived[:, :columns]).astype(BF16)
    answered[...] = jnp.zeros_like(answered)
    copies[0].wait()
    copies[1].start()
    copies[2].start()
    factor = (1.0 / math.sqrt(HEAD_WIDTH))

    def chunk_step(index, carry):
        base = pl.multiple_of(index * CHUNK, CHUNK)
        parent = jnp.int32(0)
        for end in ends[:-1]:
            parent = parent + (base >= end).astype(jnp.int32)
        length = lengths_ref[parent]

        def heads_of(span):
            for j in range(kv_heads):
                block = ordered[pl.ds(base, CHUNK), j * width : (j + 1) * width]
                heads = jnp.concatenate(
                    [block[:, g * HEAD_WIDTH : (g + 1) * HEAD_WIDTH] for g in range(group)], axis=0
                )
                scores = product(heads, turned_ref[parent, j, :, :span])
                raised = jnp.exp(scores * factor).astype(BF16)
                summed = product(raised, valued_ref[parent, j, :span])
                scaled = (summed[:, :HEAD_WIDTH] / summed[:, HEAD_WIDTH:]).astype(BF16)
                for g in range(group):
                    answered[
                        pl.ds(base, CHUNK),
                        j * width + g * HEAD_WIDTH : j * width + (g + 1) * HEAD_WIDTH,
                    ] = scaled[g * CHUNK : (g + 1) * CHUNK]

        for span in range(256, prefix + 1, 256):
            @pl.when((length > span - 256) & (length <= span))
            def _(span=span):
                heads_of(span)
        return carry

    lax.fori_loop(0, lax.shift_right_logical(start, CHUNK.bit_length() - 1), chunk_step, 0)
    lane = iota((slots, places), 1).astype(F32)
    back = one_hot(lane == position[:, :1])
    attended_ref[...] = product(back, answered[...]).astype(BF16)
    copies[1].wait()
    partial_ref[...] = product(attended_ref[...], weight_ref[...]).astype(BF16)
    copies[2].wait()


def project_kernel(attended_ref, weight_ref, out_ref):
    out_ref[...] = product(attended_ref[...], weight_ref[...])


def mix_kernel(capacity, parents_here, ids_ref, returned_ref, residual_ref, out_ref):
    children = residual_ref.shape[0]
    slot, _ = slots_of(ids_ref[...], parents_here, capacity)
    placing = one_hot(
        iota((children, returned_ref.shape[0]), 1) == as_column(slot).astype(jnp.int32)
    )
    found = product(placing, returned_ref[...])
    out_ref[...] = (residual_ref[...].astype(F32) + found).astype(BF16)


def local(queries, cached_key_rows, cached_value_rows, parent_ids, lengths, residual, out_weight):
    dp_count = lax.axis_size("dp")
    tensor_count = lax.axis_size("tensor")
    children, columns = queries.shape
    parents_here, prefix, key_columns = cached_key_rows.shape
    kv_heads = key_columns // HEAD_WIDTH
    capacity = max(2, 2 * children // dp_count)
    slots = dp_count * capacity
    half = out_weight.shape[1] // tensor_count
    ids = parent_ids.reshape(1, children)
    outgoing = pl.pallas_call(
        lambda *refs: send_kernel(capacity, parents_here, *refs),
        out_shape=jax.ShapeDtypeStruct((slots, columns + LANES), BF16),
        in_specs=[VMEM, VMEM],
        out_specs=VMEM,
        compiler_params=params(6),
        name="send",
    )(ids, queries)
    arrived = lax.all_to_all(
        outgoing.reshape(dp_count, capacity, columns + LANES), "dp", 0, 0, tiled=True
    )
    turned, valued = pl.pallas_call(
        prepare_kernel,
        out_shape=(
            jax.ShapeDtypeStruct((parents_here, kv_heads, HEAD_WIDTH, prefix), BF16),
            jax.ShapeDtypeStruct((parents_here, kv_heads, prefix, 2 * HEAD_WIDTH), BF16),
        ),
        in_specs=[SMEM, VMEM, VMEM],
        out_specs=(VMEM, VMEM),
        compiler_params=params(16),
        cost_estimate=pl.CostEstimate(
            flops=10000000000, bytes_accessed=4 * out_weight.size, transcendentals=0
        ),
        name="prepare",
    )(lengths, cached_key_rows, cached_value_rows)
    places = slots + (parents_here - 1) * CHUNK
    attended, partial_value, weight_mine = pl.pallas_call(
        attend_kernel,
        out_shape=(
            jax.ShapeDtypeStruct((slots, columns), BF16),
            jax.ShapeDtypeStruct((slots, half), BF16),
            jax.ShapeDtypeStruct((columns, half), BF16),
        ),
        in_specs=[SMEM, VMEM, VMEM, HBM, HBM],
        out_specs=(VMEM, VMEM, VMEM),
        scratch_shapes=[
            pltpu.VMEM((parents_here, kv_heads, prefix, 2 * HEAD_WIDTH), BF16),
            pltpu.VMEM((columns, half), BF16),
            pltpu.VMEM((places, columns), BF16),
            pltpu.VMEM((places, columns), BF16),
            pltpu.SemaphoreType.DMA((3,)),
        ],
        compiler_params=params(40),
        name="attend",
    )(
        lengths,
        arrived,
        turned,
        pltpu.with_memory_space_constraint(valued, pltpu.HBM),
        pltpu.with_memory_space_constraint(out_weight, pltpu.HBM),
    )
    other = lax.ppermute(partial_value, "tensor", [(0, 1), (1, 0)])
    mine = pl.pallas_call(
        project_kernel,
        out_shape=jax.ShapeDtypeStruct((slots, half), F32),
        in_specs=[VMEM, VMEM],
        out_specs=VMEM,
        compiler_params=params(14),
        cost_estimate=pl.CostEstimate(
            flops=2 * slots * columns * half, bytes_accessed=2 * columns * half, transcendentals=0
        ),
        name="project",
    )(attended, weight_mine)
    answers = (mine + other.astype(F32)).astype(BF16)
    returned = lax.all_to_all(
        answers.reshape(dp_count, capacity, half), "dp", 0, 0, tiled=True
    ).reshape(slots, half)
    return pl.pallas_call(
        lambda *refs: mix_kernel(capacity, parents_here, *refs),
        out_shape=jax.ShapeDtypeStruct(residual.shape, BF16),
        in_specs=[VMEM, VMEM, VMEM],
        out_specs=VMEM,
        compiler_params=params(6),
        name="mix",
    )(ids, returned, residual)


def solution(mesh):
    placed = (
        P("dp", "tensor"),
        P("dp", None, "tensor"),
        P("dp", None, "tensor"),
        P("dp"),
        P("dp"),
        P("dp", "tensor"),
        P("tensor", None),
    )
    return jax.shard_map(
        local, mesh=mesh, in_specs=placed, out_specs=P("dp", "tensor"), check_vma=False
    )
```
